128 devices in a mesh: ob: 16 (over y_hi, z, core), pt: 8 (over x, y_lo).
Axes of the slice: x: 4, y: 4 (y_hi: 2, y_lo: 2; y = y_hi * 2 + y_lo), z: 4, core: 2. Of those that a mesh axis runs over, the one named last changes fastest.
Arguments:
- orbitals: float32 [512, 262144], P(('ob', 'pt')), may hold values from -32 to 32, as said below
- potential: float32 [262144], replicated, may hold values from 0 to 2
- cutoff: float32 [1], replicated, may hold values from 0.4 to 1
- eigvec: float32 [512, 512], replicated, may hold values from -3 to 3, as said below
Outputs:
- gram: float32 [512, 512], P(('ob', 'pt'))
- hamil_sub: float32 [512, 512], P(('ob', 'pt'))
- rotated: float32 [512, 262144], P(None, ('ob', 'pt'))
- residual: float32 [512, 262144], P(None, ('ob', 'pt'))
- ritz: float32 [512], replicated
The draws below stay inside these ranges and needn't reach their ends.
Inputs may be any that keep to these rules, and one draw needn't show every extreme that they name: `orbitals`: each orbital is a rough field whose scale differs from orbital to orbital and from region to region of the grid. `eigvec`: A full-rank matrix with a unit-sized diagonal and independent off-diagonal entries.
All inputs are finite; a program needn't handle non-finite values.
Results may differ from the reference program's by a relative error of at most 0.00027.
Values sent between devices are 32-bit elements; how exact they have to be, the bound alone decides.
No kernel may reach another device: no remote copies, remote signals or barrier semaphores. Data moves between devices by JAX's collectives and lax.ppermute only.
A program may use at most 128 MiB of HBM per device.

```python
import jax
import jax.numpy as jnp
from jax import lax

G = 64
DEGREE = 12
ORB_DEV = 4
NORB = 512
NPTS = 262144


def draw_orbitals(key, part):
    key_base = jax.random.fold_in(key, 11)
    key_scale = jax.random.fold_in(key, 13)
    key_region = jax.random.fold_in(key, 14)
    points = lax.iota(jnp.int32, NPTS)
    x_coord = points // (G * G)
    y_coord = points // G % G
    z_coord = points % G
    block_id = x_coord * 8 // G * 64 + y_coord * 8 // G * 8 + z_coord * 8 // G
    base = jnp.clip(jax.random.normal(key_base, (NORB, NPTS), jnp.float32), -4.0, 4.0)
    region_table = jnp.exp(jax.random.uniform(key_region, (512,), jnp.float32, jnp.log(0.5), jnp.log(2.0)))
    orb_scale = jnp.exp(jax.random.uniform(key_scale, (NORB, 1), jnp.float32, jnp.log(0.4), jnp.log(4.0)))
    region = region_table[block_id][None, :]
    return jnp.clip(base * orb_scale * region, -32.0, 32.0)


def draw_eigvec(key, part):
    key_off = jax.random.fold_in(key, 21)
    off_diag = jnp.clip(jax.random.normal(key_off, (NORB, NORB), jnp.float32), -4.0, 4.0)
    return jnp.eye(NORB, dtype=jnp.float32) + 0.6 * off_diag / jnp.sqrt(jnp.float32(NORB))


def setup_inputs(seed: int = 0) -> dict:
    key_of = jax.random.split(jax.random.key(seed), 5)
    orbitals = draw_orbitals(jax.random.fold_in(key_of[4], 71), 0)
    potential = jnp.clip(jax.random.uniform(key_of[1], (NPTS,), jnp.float32, 0.0, 2.0), 0.0, 2.0)
    cutoff = jnp.clip(jax.random.uniform(key_of[2], (1,), jnp.float32, 0.4, 1.0), 0.4, 1.0)
    eigvec = draw_eigvec(jax.random.fold_in(key_of[4], 71), 0)
    return dict(orbitals=orbitals, potential=potential, cutoff=cutoff, eigvec=eigvec)


upper_bound = 8.0
quot_eps = 1e-6


def apply_ham(fields, potential):
    points = fields.shape[-1]
    plane_len = G * G
    x_pair = jnp.roll(fields, plane_len, axis=-1) + jnp.roll(fields, -plane_len, axis=-1)
    cube_view = fields.reshape(fields.shape[0], G, plane_len)
    y_pair = (jnp.roll(cube_view, G, axis=-1) + jnp.roll(cube_view, -G, axis=-1)).reshape(fields.shape)
    z_index = lax.broadcasted_iota(jnp.int32, (1, points), 1) % G
    z_lower = jnp.where(z_index == 0, jnp.roll(fields, 1 - G, axis=-1), jnp.roll(fields, 1, axis=-1))
    z_upper = jnp.where(z_index == G - 1, jnp.roll(fields, G - 1, axis=-1), jnp.roll(fields, -1, axis=-1))
    return -0.5 * (x_pair + y_pair + z_lower + z_upper - 6.0 * fields) + potential * fields


def chebyshev(fields, potential, cutoff):
    center = 0.5 * (upper_bound + cutoff[0])
    half_width = 0.5 * (upper_bound - cutoff[0])
    current = (apply_ham(fields, potential) - center * fields) / half_width

    def advance(turn_idx, carry):
        previous, present = carry
        following = 2.0 * (apply_ham(present, potential) - center * present) / half_width - previous
        return (present, following)

    previous, current = lax.fori_loop(0, DEGREE - 1, advance, (fields, current))
    return current, apply_ham(current, potential)


def reference(orbitals, potential, cutoff, eigvec):
    blocks = orbitals.reshape(-1, ORB_DEV, NPTS)
    filtered, applied = lax.map(lambda block: chebyshev(block, potential, cutoff), blocks)
    filtered = filtered.reshape(NORB, NPTS)
    applied = applied.reshape(NORB, NPTS)
    high = lax.Precision.HIGHEST
    gram = jnp.dot(filtered, filtered.T, precision=high) / NPTS
    hamil_sub = jnp.dot(filtered, applied.T, precision=high) / NPTS
    rotated = jnp.dot(eigvec.T, filtered, precision=high)
    rot_applied = jnp.dot(eigvec.T, applied, precision=high)
    numer = jnp.sum(eigvec * jnp.dot(hamil_sub, eigvec, precision=high), axis=0)
    denom = jnp.sum(eigvec * jnp.dot(gram, eigvec, precision=high), axis=0)
    ritz = numer / (denom + quot_eps)
    residual = rot_applied - ritz[:, None] * rotated
    return (gram, hamil_sub, rotated, residual, ritz)
```

```python
import functools

import jax
import jax.numpy as jnp
from jax import lax
from jax.experimental import pallas as pl
from jax.experimental.pallas import tpu as pltpu
from jax.sharding import PartitionSpec as P

NPTS = 262144
CHUNKS = (2, 2)
AXES = ("ob", "pt")
upper_bound = 8.0
quot_eps = 1e-06

YB = 16

def lane_roll(v, s):
    n = v.shape[0]
    return pltpu.roll(v.reshape(n * 8, 128), s % 128, 1).reshape(n, 8, 128)

def sub_roll(v, s):
    return pltpu.roll(v, s % 8, 1)

def filter_kernel(first, count, x_ref, pot_ref, cut_ref, out_ref, abuf, bbuf, wbuf):
    cut = cut_ref[0]
    center = 0.5 * (upper_bound + cut)
    half_width = 0.5 * (upper_bound - cut)
    alpha = -1.0 / half_width
    lane = lax.broadcasted_iota(jnp.int32, (YB, 8, 128), 2)
    low_half = lax.broadcasted_iota(jnp.int32, (8, 128), 1) < 64
    z_first = (lane & 63) == 0
    z_last = (lane & 63) == 63

    def to_blocks(load, store):
        def body(xl, _):
            for yp in range(16):
                a = load(xl * 32 + yp)
                b = load(xl * 32 + 16 + yp)
                ra, rb = pltpu.roll(a, 64, 1), pltpu.roll(b, 64, 1)
                store(xl, 2 * yp, jnp.where(low_half, a, rb))
                store(xl, 2 * yp + 1, jnp.where(low_half, ra, b))
            return 0
        lax.fori_loop(0, 8, body, 0)

    def w_store(xl, y, v):
        wbuf[xl, y] = v * (2.0 / half_width)
    to_blocks(lambda r: pot_ref[pl.ds(r, 8, stride=256), :] + (3.0 - center), w_store)


    def halo(buf):
        for xl in range(8):
            buf[xl, 0] = pltpu.roll(buf[xl, 32], 64, 1)
            buf[xl, 33] = pltpu.roll(buf[xl, 1], 64, 1)

    def sweep(cur, emit):
        def block(yb, _):
            y0 = yb * YB
            def at(xl):
                return cur[xl, pl.ds(y0 + 1, YB)]
            below = sub_roll(at(7), 1)
            here = at(0)
            wrap = sub_roll(here, -1)
            for xl in range(8):
                above = at(xl + 1) if xl < 7 else wrap
                lo = cur[xl, pl.ds(y0, 1)]
                hi = cur[xl, pl.ds(y0 + YB + 1, 1)]
                ym = jnp.concatenate([lo, here[:YB - 1]], 0)
                yp = jnp.concatenate([here[1:], hi], 0)
                zm = jnp.where(z_first, lane_roll(here, -63), lane_roll(here, 1))
                zp = jnp.where(z_last, lane_roll(here, 63), lane_roll(here, -1))
                s = ((below + above) + (ym + yp)) + (zm + zp)
                t = alpha * s + wbuf[xl, pl.ds(y0, YB)] * here
                emit(xl, y0, here, t)
                below, here = here, above
            return 0
        lax.fori_loop(0, 32 // YB, block, 0)

    def advance(cur, old):
        def emit(xl, y0, v, t):
            old[xl, pl.ds(y0 + 1, YB)] = t - old[xl, pl.ds(y0 + 1, YB)]
        sweep(cur, emit)
        halo(old)

    def one(o, _):
        orb = first + o
        def y_store(xl, y, v):
            abuf[xl, y + 1] = v
        to_blocks(lambda r: x_ref[pl.ds(r * 4 + orb, 8, stride=1024), :], y_store)
        halo(abuf)

        def emit_first(xl, y0, v, t):
            bbuf[xl, pl.ds(y0 + 1, YB)] = 0.5 * t
        sweep(abuf, emit_first)
        halo(bbuf)

        def pair(k, _):
            advance(bbuf, abuf)
            @pl.when(k < 5)
            def _():
                advance(abuf, bbuf)
            return 0
        lax.fori_loop(0, 6, pair, 0)

        def emit_last(xl, y0, v, t):
            ap = (0.5 * half_width) * t + center * v
            yp0 = y0 // 2
            for which, val in ((0, v), (1, ap)):
                for j in range(YB // 2):
                    e, d = val[2 * j], val[2 * j + 1]
                    re, rd = pltpu.roll(e, 64, 1), pltpu.roll(d, 64, 1)
                    a = jnp.where(low_half, e, rd)
                    b = jnp.where(low_half, re, d)
                    q = (2 * o + which) * 16 + yp0 + j
                    out_ref[pl.ds(2 * xl * (32 * count) + q, 8, stride=512 * count), :] = a
                    out_ref[pl.ds((2 * xl + 1) * (32 * count) + q, 8, stride=512 * count), :] = b
        sweep(abuf, emit_last)
        return 0
    lax.fori_loop(0, count, one, 0)


def run_filter(orb, pot, cut, first, count):
    return pl.pallas_call(
        functools.partial(filter_kernel, first, count),
        out_shape=jax.ShapeDtypeStruct((128 * 2 * count * 16, 128), jnp.float32),
        in_specs=[
            pl.BlockSpec(memory_space=pltpu.VMEM),
            pl.BlockSpec(memory_space=pltpu.VMEM),
            pl.BlockSpec(memory_space=pltpu.SMEM),
        ],
        out_specs=pl.BlockSpec(memory_space=pltpu.VMEM),
        scratch_shapes=[
            pltpu.VMEM((8, 34, 8, 128), jnp.float32),
            pltpu.VMEM((8, 34, 8, 128), jnp.float32),
            pltpu.VMEM((8, 32, 8, 128), jnp.float32),
        ],
        compiler_params=pltpu.CompilerParams(vmem_limit_bytes=30 << 20),
        cost_estimate=pl.CostEstimate(
            flops=count * 13 * NPTS * 40, bytes_accessed=count << 21, transcendentals=0
        ),
        name="filter",
    )(orb, pot, cut)


def project_kernel(*refs):
    n = len(CHUNKS)
    chunks, (e_ref, rot_ref, rota_ref, pay_ref, e3, gram, hamil, acc_n, acc_d) = refs[:n], refs[n:]
    where = [(c, o) for c in range(n) for o in range(CHUNKS[c])]
    e = e_ref[...]
    e_hi = e.astype(jnp.bfloat16)
    e3[:, :512] = e_hi
    e3[:, 512:1024] = e_hi
    e3[:, 1024:] = (e - e_hi.astype(jnp.float32)).astype(jnp.bfloat16)
    gram[...] = jnp.zeros_like(gram)
    hamil[...] = jnp.zeros_like(hamil)
    acc_n[...] = jnp.zeros_like(acc_n)
    acc_d[...] = jnp.zeros_like(acc_d)

    def fetch(t, which):
        cols = []
        for h in range(2):
            rows = []
            for c, o in where:
                rows.append(
                    chunks[c][pl.ds((2 * o + which) * 16 + 2 * t + h, 128, stride=32 * CHUNKS[c]), :]
                )
            cols.append(jnp.concatenate(rows, 0))
        x = jnp.concatenate(cols, 1)
        hi = x.astype(jnp.bfloat16)
        lo = (x - hi.astype(jnp.float32)).astype(jnp.bfloat16)
        return hi, lo

    def nt(a, b):
        return lax.dot_general(a, b, (((1,), (1,)), ((), ())), preferred_element_type=jnp.float32)

    def body(t, _):
        fh, fl = fetch(t, 0)
        ah, al = fetch(t, 1)
        left = jnp.concatenate([fh, fh, fl], 1)
        gram[...] += nt(left, jnp.concatenate([fh, fl, fh], 1))
        hamil[...] += nt(left, jnp.concatenate([ah, al, ah], 1))
        rot = jnp.dot(e3[...], jnp.concatenate([fh, fl, fh], 0), preferred_element_type=jnp.float32)
        rota = jnp.dot(e3[...], jnp.concatenate([ah, al, ah], 0), preferred_element_type=jnp.float32)
        cols = pl.ds(pl.multiple_of(t * 256, 256), 256)
        rot_ref[:, cols] = rot
        rota_ref[:, cols] = rota
        pn, pd = rot * rota, rot * rot
        acc_n[...] += pn[:, :128] + pn[:, 128:]
        acc_d[...] += pd[:, :128] + pd[:, 128:]
        return 0

    lax.fori_loop(0, 8, body, 0)
    scale = 1.0 / NPTS
    for m, mat in enumerate((gram, hamil)):
        for o in range(4):
            for q in range(4):
                pay_ref[pl.ds(m * 16 + o * 4 + q, 128, stride=40), :] = (
                    mat[128 * o : 128 * o + 128, 128 * q : 128 * q + 128] * scale
                )
    for m, acc in enumerate((acc_n, acc_d)):
        for q in range(4):
            row = jnp.sum(acc[128 * q : 128 * q + 128, :].T, axis=0, keepdims=True) * scale
            pay_ref[pl.ds(32 + m * 4 + q, 128, stride=40), :] = jnp.broadcast_to(row, (128, 128))


def run_project(chunks, et):
    vm = pl.BlockSpec(memory_space=pltpu.VMEM)
    return pl.pallas_call(
        project_kernel,
        out_shape=(
            jax.ShapeDtypeStruct((512, 2048), jnp.float32),
            jax.ShapeDtypeStruct((512, 2048), jnp.float32),
            jax.ShapeDtypeStruct((128 * 40, 128), jnp.float32),
        ),
        in_specs=[vm] * (len(chunks) + 1),
        out_specs=(vm, vm, vm),
        scratch_shapes=[
            pltpu.VMEM((512, 1536), jnp.bfloat16),
            pltpu.VMEM((512, 512), jnp.float32),
            pltpu.VMEM((512, 512), jnp.float32),
            pltpu.VMEM((512, 128), jnp.float32),
            pltpu.VMEM((512, 128), jnp.float32),
        ],
        compiler_params=pltpu.CompilerParams(vmem_limit_bytes=50 << 20),
        cost_estimate=pl.CostEstimate(flops=13 << 30, bytes_accessed=20 << 20, transcendentals=0),
        name="project",
    )(*chunks, et)


def on_device(orbitals, potential, cutoff, eigvec):
    orb = orbitals.reshape(4, 2048, 128).transpose(1, 0, 2).reshape(8192, 128)
    pot = potential.reshape(2048, 128)
    et = eigvec.reshape(128, 4, 512).transpose(2, 1, 0).reshape(512, 512)
    received = []
    first = 0
    for count in CHUNKS:
        sent = run_filter(orb, pot, cutoff, first, count).reshape(128, 32 * count, 128)
        got = lax.all_to_all(sent, AXES, split_axis=0, concat_axis=0, tiled=True)
        received.append(got.reshape(128 * 32 * count, 128))
        first += count
    rotated, rot_applied, pay = run_project(received, et)
    pay = lax.all_to_all(pay.reshape(128, 40, 128), AXES, split_axis=0, concat_axis=0, tiled=True)
    total = jnp.sum(pay, axis=0)
    mats = total[:32].reshape(2, 4, 4, 128).transpose(0, 1, 3, 2).reshape(2, 4, 512)
    numer = total[32:36].reshape(512)
    denom = total[36:40].reshape(512)
    ritz = numer / (denom + quot_eps)
    residual = rot_applied - ritz[:, None] * rotated
    return (mats[0], mats[1], rotated, residual, ritz)


def solution(mesh):
    return jax.shard_map(
        on_device,
        mesh=mesh,
        in_specs=(P(AXES, None), P(), P(), P()),
        out_specs=(P(AXES, None), P(AXES, None), P(None, AXES), P(None, AXES), P()),
        check_vma=False,
    )
```

```python
import functools

import jax
import jax.numpy as jnp
import numpy as np
from jax import lax
from jax.experimental import pallas as pl
from jax.experimental.pallas import tpu as pltpu
from jax.sharding import PartitionSpec as P

NPTS = 262144
TILE = 512
AXES = ("oh", "core", "pt")
upper_bound = 8.0
quot_eps = 1e-06


def split3(v):
    hi = v.astype(jnp.bfloat16)
    rest = v - hi.astype(jnp.float32)
    mid = rest.astype(jnp.bfloat16)
    lo = (rest - mid.astype(jnp.float32)).astype(jnp.bfloat16)
    return jnp.concatenate([hi, mid, lo], 1)


def shifted(vs, k):
    return [pltpu.roll(v, k, 1) for v in vs]


def added(xs, ys):
    return [x + y for x, y in zip(xs, ys)]


def filter_kernel(
    first, count, orb_ref, pot_ref, cut_ref, out_ref, abuf, bbuf, wbuf, nat, filt, appl, perm, back, in_sem, out_sem
):
    cut = cut_ref[0]
    center = 0.5 * (upper_bound + cut)
    half_width = 0.5 * (upper_bound - cut)
    alpha = -1.0 / half_width
    odd_lane = (lax.broadcasted_iota(jnp.int32, (8, 128), 1) & 1) == 1
    row = lax.broadcasted_iota(jnp.int32, (256, 256), 0)
    col = lax.broadcasted_iota(jnp.int32, (256, 256), 1)

    def target(k):
        return ((k >> 6) & 1) * 128 + (k & 63) * 2 + (k >> 7)

    for part in range(3):
        perm[256 * part : 256 * part + 256, :] = jnp.where(target(row) == col, 1.0, 0.0).astype(jnp.bfloat16)
        back[256 * part : 256 * part + 256, :] = jnp.where(target(col) == row, 1.0, 0.0).astype(jnp.bfloat16)

    filt16 = filt.reshape(16, 16, 8, 128)
    appl16 = appl.reshape(16, 16, 8, 128)

    def orb_copy(o, s):
        return pltpu.make_async_copy(
            orb_ref.at[s, :, :, first + o, :], nat.at[o % 2, :, :, s, :], in_sem.at[o % 2, s]
        )

    def pot_copy(s):
        return pltpu.make_async_copy(pot_ref.at[s], nat.at[1, :, :, s, :], in_sem.at[1, s])

    def out_copies(o, s):
        return (
            pltpu.make_async_copy(filt16.at[:, :, s, :], out_ref.at[s, :, 2 * o, :, :], out_sem.at[0, s]),
            pltpu.make_async_copy(appl16.at[:, :, s, :], out_ref.at[s, :, 2 * o + 1, :, :], out_sem.at[1, s]),
        )

    def to_blocks(slot, store):
        def body(h, _):
            x0 = 4 * h
            a = nat[slot, pl.ds(x0, 4), :16].reshape(512, 128)
            b = nat[slot, pl.ds(x0, 4), 16:].reshape(512, 128)
            v = jnp.dot(split3(jnp.concatenate([a, b], 1)), perm[...], preferred_element_type=jnp.float32)
            even = v[:, :128].reshape(4, 16, 8, 128)
            odd = v[:, 128:].reshape(4, 16, 8, 128)
            for i in range(4):
                for yp in range(16):
                    store(x0 + i, 2 * yp, even[i, yp])
                    store(x0 + i, 2 * yp + 1, odd[i, yp])
            return 0

        lax.fori_loop(0, 2, body, 0)

    def to_natural(buf, out):
        def body(h, _):
            x0 = 4 * h
            rows = [
                jnp.concatenate([buf[x0 + i, 2 * yp + p] for i in range(4) for yp in range(16)], 0) for p in range(2)
            ]
            v = jnp.dot(split3(jnp.concatenate(rows, 1)), back[...], preferred_element_type=jnp.float32)
            out[pl.ds(x0, 4), :16] = v[:, :128].reshape(4, 16, 8, 128)
            out[pl.ds(x0, 4), 16:] = v[:, 128:].reshape(4, 16, 8, 128)
            return 0

        lax.fori_loop(0, 2, body, 0)

    def flip(v):
        return jnp.where(odd_lane, pltpu.roll(v, 1, 1), pltpu.roll(v, 127, 1))

    def sweep(cur, emit):
        def at(xl):
            return [cur[xl, y] for y in range(32)]

        below = [pltpu.roll(v, 1, 0) for v in at(7)]
        here = at(0)
        wrap = [pltpu.roll(v, 7, 0) for v in here]
        for xl in range(8):
            above = at(xl + 1) if xl < 7 else wrap
            ring = [flip(here[31])] + here + [flip(here[0])]
            zs = added(shifted(here, 2), shifted(here, 126))
            s = added(added(added(below, above), added(ring[:32], ring[2:])), zs)
            emit(xl, here, [alpha * s[y] + wbuf[xl, y] * here[y] for y in range(32)])
            below, here = here, above

    def advance(cur, old):
        def emit(xl, v, t):
            prev = [old[xl, y] for y in range(32)]
            for y in range(32):
                old[xl, y] = t[y] - prev[y]

        sweep(cur, emit)

    for s in range(8):
        pot_copy(s).start()
        orb_copy(0, s).start()
    for s in range(8):
        pot_copy(s).wait()

    def w_store(xl, y, v):
        wbuf[xl, y] = (v + (3.0 - center)) * (2.0 / half_width)

    to_blocks(1, w_store)

    def one(o, _):
        for s in range(8):
            orb_copy(o, s).wait()

        @pl.when(o + 1 < count)
        def _():
            for s in range(8):
                orb_copy(o + 1, s).start()

        def y_store(xl, y, v):
            abuf[xl, y] = v

        to_blocks(o % 2, y_store)

        def emit_first(xl, v, t):
            for y in range(32):
                bbuf[xl, y] = 0.5 * t[y]

        sweep(abuf, emit_first)

        def pair(k, _):
            advance(bbuf, abuf)

            @pl.when(k < 5)
            def _():
                advance(abuf, bbuf)

            return 0

        lax.fori_loop(0, 6, pair, 0)

        @pl.when(o > 0)
        def _():
            for s in range(8):
                for copy in out_copies(o - 1, s):
                    copy.wait()

        def emit_last(xl, v, t):
            for y in range(32):
                bbuf[xl, y] = (0.5 * half_width) * t[y] + center * v[y]

        sweep(abuf, emit_last)
        to_natural(abuf, filt)
        to_natural(bbuf, appl)
        for s in range(8):
            for copy in out_copies(o, s):
                copy.start()
        return 0

    lax.fori_loop(0, count, one, 0)
    for s in range(8):
        for copy in out_copies(count - 1, s):
            copy.wait()


def run_filter(orb, pot, cut, first, count):
    return pl.pallas_call(
        functools.partial(filter_kernel, first, count),
        out_shape=jax.ShapeDtypeStruct((8, 16, 2 * count, 16, 128), jnp.float32),
        in_specs=[
            pl.BlockSpec(memory_space=pl.ANY),
            pl.BlockSpec(memory_space=pl.ANY),
            pl.BlockSpec(memory_space=pltpu.SMEM),
        ],
        out_specs=pl.BlockSpec(memory_space=pl.ANY),
        scratch_shapes=[
            pltpu.VMEM((8, 32, 8, 128), jnp.float32),
            pltpu.VMEM((8, 32, 8, 128), jnp.float32),
            pltpu.VMEM((8, 32, 8, 128), jnp.float32),
            pltpu.VMEM((2, 8, 32, 8, 128), jnp.float32),
            pltpu.VMEM((8, 32, 8, 128), jnp.float32),
            pltpu.VMEM((8, 32, 8, 128), jnp.float32),
            pltpu.VMEM((768, 256), jnp.bfloat16),
            pltpu.VMEM((768, 256), jnp.bfloat16),
            pltpu.SemaphoreType.DMA((2, 8)),
            pltpu.SemaphoreType.DMA((2, 8)),
        ],
        compiler_params=pltpu.CompilerParams(vmem_limit_bytes=60 << 20),
        cost_estimate=pl.CostEstimate(
            flops=count * 13 * NPTS * 2000, bytes_accessed=count << 21, transcendentals=0
        ),
        name="filter",
    )(orb, pot, cut)


def halves(v):
    hi = v.astype(jnp.bfloat16)
    return hi, (v - hi.astype(jnp.float32)).astype(jnp.bfloat16)


def nt(a, b):
    return lax.dot_general(a, b, (((1,), (1,)), ((), ())), preferred_element_type=jnp.float32)


def nn(a, b):
    return jnp.dot(a, b, preferred_element_type=jnp.float32)


def tile_copies(got_ref, xbuf, sems, t):
    copies = []
    for which in range(2):
        for o in range(2):
            for c in range(TILE // 128):
                copies.append(
                    pltpu.make_async_copy(
                        got_ref.at[:, (2 * o + which) * 16 + t * (TILE // 128) + c, :],
                        xbuf.at[t % 2, which, pl.ds(128 * o, 128), pl.ds(128 * c, 128)],
                        sems.at[t % 2, len(copies)],
                    )
                )
    return copies


def load_tile(got_ref, xbuf, sems):
    t = pl.program_id(0)

    @pl.when(t == 0)
    def _():
        for copy in tile_copies(got_ref, xbuf, sems, t):
            copy.start()

    @pl.when(t + 1 < pl.num_programs(0))
    def _():
        for copy in tile_copies(got_ref, xbuf, sems, t + 1):
            copy.start()

    for copy in tile_copies(got_ref, xbuf, sems, t):
        copy.wait()
    return halves(xbuf[t % 2, 0]), halves(xbuf[t % 2, 1])


def split_e(e_ref, e3, first):
    hi, lo = halves(e_ref[:, first : first + 256])
    e3[:, :256] = hi
    e3[:, 256:512] = hi
    e3[:, 512:] = lo


def project_first(got_ref, e_ref, rot_ref, rota_ref, fh_ref, fl_ref, mat_ref, e3, xbuf, sems):
    @pl.when(pl.program_id(0) == 0)
    def _():
        split_e(e_ref, e3, 0)
        mat_ref[...] = jnp.zeros_like(mat_ref)

    (fh, fl), (ah, al) = load_tile(got_ref, xbuf, sems)
    fh_ref[...] = fh
    fl_ref[...] = fl
    rot_ref[...] = nn(e3[...], jnp.concatenate([fh, fl, fh], 0))
    rota_ref[...] = nn(e3[...], jnp.concatenate([ah, al, ah], 0))
    right = jnp.concatenate([jnp.concatenate([fh, fl, fh], 1), jnp.concatenate([ah, al, ah], 1)], 0)
    mat_ref[...] += nt(jnp.concatenate([fh, fh, fl], 1), right)


def project_last(
    got_ref, e_ref, rot0_ref, rota0_ref, f0h_ref, f0l_ref, mat0_ref, core_ref,
    rot_ref, rota_ref, keep_ref, send_ref, e3, xbuf, mat, acc_n, acc_d, sems,
):
    @pl.when(pl.program_id(0) == 0)
    def _():
        split_e(e_ref, e3, 256)
        mat[...] = jnp.zeros_like(mat)
        acc_n[...] = jnp.zeros_like(acc_n)
        acc_d[...] = jnp.zeros_like(acc_d)

    (fh, fl), (ah, al) = load_tile(got_ref, xbuf, sems)
    f0h, f0l = f0h_ref[...], f0l_ref[...]
    left = jnp.concatenate([jnp.concatenate([f0h, f0h, f0l], 1), jnp.concatenate([fh, fh, fl], 1)], 0)
    right = jnp.concatenate([jnp.concatenate([fh, fl, fh], 1), jnp.concatenate([ah, al, ah], 1)], 0)
    mat[...] += nt(left, right)
    rot = rot0_ref[...] + nn(e3[...], jnp.concatenate([fh, fl, fh], 0))
    rota = rota0_ref[...] + nn(e3[...], jnp.concatenate([ah, al, ah], 0))
    rot_ref[...] = rot
    rota_ref[...] = rota
    pn, pd = rot * rota, rot * rot
    acc_n[...] += sum(pn[:, 128 * c : 128 * c + 128] for c in range(TILE // 128))
    acc_d[...] += sum(pd[:, 128 * c : 128 * c + 128] for c in range(TILE // 128))

    @pl.when(pl.program_id(0) == pl.num_programs(0) - 1)
    def _():
        scale = 1.0 / NPTS
        me = core_ref[0]
        rows = []
        for m in range(2):
            here = slice(256 * m, 256 * m + 256)
            upper = mat[:256, here]
            rows.append(jnp.concatenate([mat0_ref[:, here], upper], 1) * scale)
            rows.append(jnp.concatenate([upper.T, mat[256:, here]], 1) * scale)
        sums = []
        for acc in (acc_n, acc_d):
            for q in range(4):
                sums.append(jnp.sum(acc[128 * q : 128 * q + 128, :].T, axis=0, keepdims=True) * scale)

        def put(ref, core):
            for oh in range(8):
                src = oh * 16 + core * 8
                base = oh * 8 * 40
                for m in range(2):
                    for o in range(4):
                        block = rows[2 * m + o // 2]
                        r0 = (o % 2) * 128 + src
                        for q in range(4):
                            ref[pl.ds(base + m * 16 + o * 4 + q, 8, stride=40), :] = block[
                                r0 : r0 + 8, 128 * q : 128 * q + 128
                            ]
                for k in range(8):
                    ref[pl.ds(base + 32 + k, 8, stride=40), :] = jnp.broadcast_to(sums[k], (8, 128))

        for core in range(2):

            @pl.when(me == core)
            def _():
                put(keep_ref, core)
                put(send_ref, 1 - core)


def run_projects(got0, got1, et, core):
    f32, bf16 = jnp.float32, jnp.bfloat16
    steps = 2048 // TILE
    hbm = pl.BlockSpec(memory_space=pl.ANY)
    cols = pl.BlockSpec((512, TILE), lambda t: (0, t))
    fcols = pl.BlockSpec((256, TILE), lambda t: (0, t))

    def whole(*shape):
        return pl.BlockSpec(shape, lambda t: (0,) * len(shape))

    full = jax.ShapeDtypeStruct((512, 2048), f32)
    part = jax.ShapeDtypeStruct((256, 2048), bf16)
    scratch = [pltpu.VMEM((512, 768), bf16), pltpu.VMEM((2, 2, 256, TILE), f32)]
    sems = pltpu.SemaphoreType.DMA((2, 4 * TILE // 128))
    first = pl.pallas_call(
        project_first,
        grid=(steps,),
        out_shape=(full, full, part, part, jax.ShapeDtypeStruct((256, 512), f32)),
        in_specs=[hbm, whole(512, 512)],
        out_specs=(cols, cols, fcols, fcols, whole(256, 512)),
        scratch_shapes=scratch + [sems],
        compiler_params=pltpu.CompilerParams(vmem_limit_bytes=40 << 20),
        cost_estimate=pl.CostEstimate(flops=8 << 30, bytes_accessed=16 << 20, transcendentals=0),
        name="project_first",
    )(got0, et)
    return pl.pallas_call(
        project_last,
        grid=(steps,),
        out_shape=(full, full) + (jax.ShapeDtypeStruct((64 * 40, 128), f32),) * 2,
        in_specs=[hbm, whole(512, 512), cols, cols, fcols, fcols, whole(256, 512), pl.BlockSpec(memory_space=pltpu.SMEM)],
        out_specs=(cols, cols, whole(64 * 40, 128), whole(64 * 40, 128)),
        scratch_shapes=scratch
        + [pltpu.VMEM((512, 512), f32), pltpu.VMEM((512, 128), f32), pltpu.VMEM((512, 128), f32), sems],
        compiler_params=pltpu.CompilerParams(vmem_limit_bytes=40 << 20),
        cost_estimate=pl.CostEstimate(flops=8 << 30, bytes_accessed=24 << 20, transcendentals=0),
        name="project_last",
    )(got1, et, *first, core)


def on_device(orbitals, potential, cutoff, eigvec):
    orb = orbitals.reshape(4, 2048, 128).transpose(1, 0, 2).reshape(8, 8, 32, 4, 128)
    pot = potential.reshape(8, 8, 32, 128)
    et = eigvec.reshape(128, 4, 512).transpose(2, 1, 0).reshape(512, 512)
    got = []
    for first in (0, 2):
        sent = run_filter(orb, pot, cutoff, first, 2).reshape(128, 64, 128)
        got.append(lax.all_to_all(sent, AXES, split_axis=0, concat_axis=0, tiled=True))
    core = lax.axis_index("core").astype(jnp.int32).reshape(1)
    rotated, rot_applied, keep, send = run_projects(got[0], got[1], et, core)
    pay = keep + lax.ppermute(send, "core", [(0, 1), (1, 0)])
    pay = lax.all_to_all(pay.reshape(64, 40, 128), ("oh", "pt"), split_axis=0, concat_axis=0, tiled=True)
    total = jnp.sum(pay, axis=0)
    mats = total[:32].reshape(2, 4, 4, 128).transpose(0, 1, 3, 2).reshape(2, 4, 512)
    numer = total[32:36].reshape(512)
    denom = total[36:40].reshape(512)
    ritz = numer / (denom + quot_eps)
    residual = rot_applied - ritz[:, None] * rotated
    return (mats[0], mats[1], rotated, residual, ritz)


def solution(mesh):
    fine = jax.sharding.Mesh(np.asarray(mesh.devices).reshape(8, 2, 8), AXES)
    return jax.shard_map(
        on_device,
        mesh=fine,
        in_specs=(P(AXES, None), P(), P(), P()),
        out_specs=(P(AXES, None), P(AXES, None), P(None, AXES), P(None, AXES), P()),
        check_vma=False,
    )
```

```python
import functools

import jax
import jax.numpy as jnp
import numpy as np
from jax import lax
from jax.experimental import pallas as pl
from jax.experimental.pallas import tpu as pltpu
from jax.sharding import PartitionSpec as P

NPTS = 262144
TILE = 512
FINISH = 64
CHUNKS = (2, 2)
AXES = ("oh", "core", "pt")
upper_bound = 8.0
quot_eps = 1e-06


def split3(v):
    hi = v.astype(jnp.bfloat16)
    rest = v - hi.astype(jnp.float32)
    mid = rest.astype(jnp.bfloat16)
    lo = (rest - mid.astype(jnp.float32)).astype(jnp.bfloat16)
    return jnp.concatenate([hi, mid, lo], 1)


def shifted(vs, k):
    return [pltpu.roll(v, k, 1) for v in vs]


def added(xs, ys):
    return [x + y for x, y in zip(xs, ys)]


def filter_kernel(
    first, count, orb_ref, pot_ref, cut_ref, out_ref, abuf, bbuf, wbuf, nat, filt, appl, perm, back, in_sem, out_sem
):
    cut = cut_ref[0]
    center = 0.5 * (upper_bound + cut)
    half_width = 0.5 * (upper_bound - cut)
    alpha = -1.0 / half_width
    odd_lane = (lax.broadcasted_iota(jnp.int32, (8, 128), 1) & 1) == 1
    row = lax.broadcasted_iota(jnp.int32, (256, 256), 0)
    col = lax.broadcasted_iota(jnp.int32, (256, 256), 1)

    def target(k):
        return ((k >> 6) & 1) * 128 + (k & 63) * 2 + (k >> 7)

    for part in range(3):
        perm[256 * part : 256 * part + 256, :] = jnp.where(target(row) == col, 1.0, 0.0).astype(jnp.bfloat16)
        back[256 * part : 256 * part + 256, :] = jnp.where(target(col) == row, 1.0, 0.0).astype(jnp.bfloat16)

    filt16 = filt.reshape(16, 16, 8, 128)
    appl16 = appl.reshape(16, 16, 8, 128)

    def orb_copy(o, s):
        return pltpu.make_async_copy(
            orb_ref.at[s, :, :, first + o, :], nat.at[o % 2, :, :, s, :], in_sem.at[o % 2, s]
        )

    def pot_copy(s):
        return pltpu.make_async_copy(pot_ref.at[s], nat.at[1, :, :, s, :], in_sem.at[1, s])

    def out_copy(o, which, s):
        src = (filt16, appl16)[which].at[:, :, s, :]
        return pltpu.make_async_copy(src, out_ref.at[s, :, 2 * o + which, :, :], out_sem.at[which, s])

    def to_blocks(slot, store):
        def body(h, _):
            x0 = 4 * h
            a = nat[slot, pl.ds(x0, 4), :16].reshape(512, 128)
            b = nat[slot, pl.ds(x0, 4), 16:].reshape(512, 128)
            v = jnp.dot(split3(jnp.concatenate([a, b], 1)), perm[...], preferred_element_type=jnp.float32)
            even = v[:, :128].reshape(4, 16, 8, 128)
            odd = v[:, 128:].reshape(4, 16, 8, 128)
            for i in range(4):
                for yp in range(16):
                    store(x0 + i, 2 * yp, even[i, yp])
                    store(x0 + i, 2 * yp + 1, odd[i, yp])
            return 0

        lax.fori_loop(0, 2, body, 0)

    def to_natural(buf, out):
        def body(h, _):
            x0 = 4 * h
            rows = [
                jnp.concatenate([buf[x0 + i, 2 * yp + p] for i in range(4) for yp in range(16)], 0) for p in range(2)
            ]
            v = jnp.dot(split3(jnp.concatenate(rows, 1)), back[...], preferred_element_type=jnp.float32)
            out[pl.ds(x0, 4), :16] = v[:, :128].reshape(4, 16, 8, 128)
            out[pl.ds(x0, 4), 16:] = v[:, 128:].reshape(4, 16, 8, 128)
            return 0

        lax.fori_loop(0, 2, body, 0)

    def flip(v):
        return jnp.where(odd_lane, pltpu.roll(v, 1, 1), pltpu.roll(v, 127, 1))

    def sweep(cur, emit):
        def at(xl):
            return [cur[xl, y] for y in range(32)]

        below = [pltpu.roll(v, 1, 0) for v in at(7)]
        here = at(0)
        wrap = [pltpu.roll(v, 7, 0) for v in here]
        for xl in range(8):
            above = at(xl + 1) if xl < 7 else wrap
            ring = [flip(here[31])] + here + [flip(here[0])]
            zs = added(shifted(here, 2), shifted(here, 126))
            s = added(added(added(below, above), added(ring[:32], ring[2:])), zs)
            emit(xl, here, [alpha * s[y] + wbuf[xl, y] * here[y] for y in range(32)])
            below, here = here, above

    def advance(cur, old):
        def emit(xl, v, t):
            prev = [old[xl, y] for y in range(32)]
            for y in range(32):
                old[xl, y] = t[y] - prev[y]

        sweep(cur, emit)

    for s in range(8):
        pot_copy(s).start()
        orb_copy(0, s).start()
    for s in range(8):
        pot_copy(s).wait()

    def w_store(xl, y, v):
        wbuf[xl, y] = (v + (3.0 - center)) * (2.0 / half_width)

    to_blocks(1, w_store)

    def one(o, _):
        for s in range(8):
            orb_copy(o, s).wait()

        @pl.when(o + 1 < count)
        def _():
            for s in range(8):
                orb_copy(o + 1, s).start()

        def y_store(xl, y, v):
            abuf[xl, y] = v

        to_blocks(o % 2, y_store)

        def emit_first(xl, v, t):
            for y in range(32):
                bbuf[xl, y] = 0.5 * t[y]

        sweep(abuf, emit_first)

        def pair(k, _):
            advance(bbuf, abuf)

            @pl.when(k < 5)
            def _():
                advance(abuf, bbuf)

            return 0

        lax.fori_loop(0, 6, pair, 0)

        @pl.when(o > 0)
        def _():
            for s in range(8):
                out_copy(o - 1, 0, s).wait()
                out_copy(o - 1, 1, s).wait()

        def emit_last(xl, v, t):
            for y in range(32):
                bbuf[xl, y] = (0.5 * half_width) * t[y] + center * v[y]

        to_natural(abuf, filt)
        for s in range(8):
            out_copy(o, 0, s).start()
        sweep(abuf, emit_last)
        to_natural(bbuf, appl)
        for s in range(8):
            out_copy(o, 1, s).start()
        return 0

    lax.fori_loop(0, count, one, 0)
    for s in range(8):
        out_copy(count - 1, 0, s).wait()
        out_copy(count - 1, 1, s).wait()


def run_filter(orb, pot, cut, first, count):
    return pl.pallas_call(
        functools.partial(filter_kernel, first, count),
        out_shape=jax.ShapeDtypeStruct((8, 16, 2 * count, 16, 128), jnp.float32),
        in_specs=[
            pl.BlockSpec(memory_space=pl.ANY),
            pl.BlockSpec(memory_space=pl.ANY),
            pl.BlockSpec(memory_space=pltpu.SMEM),
        ],
        out_specs=pl.BlockSpec(memory_space=pl.ANY),
        scratch_shapes=[
            pltpu.VMEM((8, 32, 8, 128), jnp.float32),
            pltpu.VMEM((8, 32, 8, 128), jnp.float32),
            pltpu.VMEM((8, 32, 8, 128), jnp.float32),
            pltpu.VMEM((2, 8, 32, 8, 128), jnp.float32),
            pltpu.VMEM((8, 32, 8, 128), jnp.float32),
            pltpu.VMEM((8, 32, 8, 128), jnp.float32),
            pltpu.VMEM((768, 256), jnp.bfloat16),
            pltpu.VMEM((768, 256), jnp.bfloat16),
            pltpu.SemaphoreType.DMA((2, 8)),
            pltpu.SemaphoreType.DMA((2, 8)),
        ],
        compiler_params=pltpu.CompilerParams(vmem_limit_bytes=60 << 20),
        cost_estimate=pl.CostEstimate(
            flops=count * 13 * NPTS * 2000, bytes_accessed=count << 21, transcendentals=0
        ),
        name="filter",
    )(orb, pot, cut)


def halves(v):
    hi = v.astype(jnp.bfloat16)
    return hi, (v - hi.astype(jnp.float32)).astype(jnp.bfloat16)


def nt(a, b):
    return lax.dot_general(a, b, (((1,), (1,)), ((), ())), preferred_element_type=jnp.float32)


def nn(a, b):
    return jnp.dot(a, b, preferred_element_type=jnp.float32)


def tile_copies(got_refs, counts, xbuf, sems, t):
    copies = []
    for which in range(2):
        row = 0
        for got_ref, count in zip(got_refs, counts):
            for o in range(count):
                for c in range(TILE // 128):
                    copies.append(
                        pltpu.make_async_copy(
                            got_ref.at[:, (2 * o + which) * 16 + t * (TILE // 128) + c, :],
                            xbuf.at[t % 2, which, pl.ds(row, 128), pl.ds(128 * c, 128)],
                            sems.at[t % 2, len(copies)],
                        )
                    )
                row += 128
    return copies


def load_tile(got_refs, counts, xbuf, sems):
    t = pl.program_id(0)

    @pl.when(t == 0)
    def _():
        for copy in tile_copies(got_refs, counts, xbuf, sems, t):
            copy.start()

    @pl.when(t + 1 < pl.num_programs(0))
    def _():
        for copy in tile_copies(got_refs, counts, xbuf, sems, t + 1):
            copy.start()

    for copy in tile_copies(got_refs, counts, xbuf, sems, t):
        copy.wait()
    return halves(xbuf[t % 2, 0]), halves(xbuf[t % 2, 1])


def in_hbm(*arrays):
    return [pltpu.with_memory_space_constraint(x, pltpu.HBM) for x in arrays]


def beside(parts, axis):
    return parts[0] if len(parts) == 1 else jnp.concatenate(parts, axis)


def full_rows(mats, m, i):
    starts = [128 * sum(CHUNKS[:k]) for k in range(len(CHUNKS) + 1)]

    def upper(i, k):
        width = 128 * CHUNKS[k]
        return mats[k][starts[i] : starts[i + 1], m * width : (m + 1) * width]

    return jnp.concatenate([upper(i, k) if k >= i else upper(k, i).T for k in range(len(CHUNKS))], 1)


def overlap_kernel(k, *refs):
    refs = list(refs)

    def take(n):
        out, refs[:] = refs[:n], refs[n:]
        return out

    count, last = CHUNKS[k], k == len(CHUNKS) - 1
    got_ref, *before = take(1 + 2 * k)
    if last:
        mats0 = take(k)
        e_ref, core_ref, keep_ref, send_ref, mat = take(5)
    else:
        fh_ref, fl_ref, mat = take(3)
    xbuf, sems = take(2)

    @pl.when(pl.program_id(0) == 0)
    def _():
        mat[...] = jnp.zeros_like(mat)

    (fh, fl), (ah, al) = load_tile([got_ref], [count], xbuf, sems)
    rows = [(before[2 * i][...], before[2 * i + 1][...]) for i in range(k)] + [(fh, fl)]
    left = beside([jnp.concatenate([h, h, l], 1) for h, l in rows], 0)
    right = jnp.concatenate([jnp.concatenate([fh, fl, fh], 1), jnp.concatenate([ah, al, ah], 1)], 0)
    mat[...] += nt(left, right)
    if not last:
        fh_ref[...] = fh
        fl_ref[...] = fl
        return

    @pl.when(pl.program_id(0) == pl.num_programs(0) - 1)
    def _():
        me = core_ref[0]
        mats = [ref[...] * (1.0 / NPTS) for ref in mats0] + [mat[...] * (1.0 / NPTS)]
        blocks = [[full_rows(mats, m, i) for i in range(len(CHUNKS))] for m in range(2)]
        where = [(i, o) for i in range(len(CHUNKS)) for o in range(CHUNKS[i])]
        e = e_ref[...]
        eh, el = halves(e)
        e3 = jnp.concatenate([eh, eh, el], 1)
        sums = []
        for m in (1, 0):
            h, l = halves(jnp.concatenate(blocks[m], 0))
            p = nn(e3, jnp.concatenate([h, l, h], 0)) * e
            acc = (p[:, :128] + p[:, 128:256]) + (p[:, 256:384] + p[:, 384:])
            for q in range(4):
                sums.append(jnp.sum(acc[128 * q : 128 * q + 128, :].T, axis=0, keepdims=True))
        sums = jnp.concatenate(sums, 0)

        def put(ref, core):
            for oh in range(8):
                base = oh * 8 * 40
                for m in range(2):
                    for o in range(4):
                        i, inner = where[o]
                        r0 = inner * 128 + oh * 16 + core * 8
                        for q in range(4):
                            ref[pl.ds(base + m * 16 + o * 4 + q, 8, stride=40), :] = blocks[m][i][
                                r0 : r0 + 8, 128 * q : 128 * q + 128
                            ]
                for pt in range(8):
                    ref[pl.ds(base + pt * 40 + 32, 8), :] = sums

        for core in range(2):

            @pl.when(me == core)
            def _():
                put(keep_ref, core)
                put(send_ref, 1 - core)


def cols(n):
    return pl.BlockSpec((n, TILE), lambda t: (0, t))


def whole(*shape):
    return pl.BlockSpec(shape, lambda t: (0,) * len(shape))


def run_overlap(k, got, before, mats, et, core):
    f32, bf16 = jnp.float32, jnp.bfloat16
    count, last = CHUNKS[k], k == len(CHUNKS) - 1
    mat_shape = (128 * sum(CHUNKS[: k + 1]), 256 * count)
    in_specs, args = [pl.BlockSpec(memory_space=pl.ANY)], [got]
    for i in range(k):
        in_specs += [cols(128 * CHUNKS[i])] * 2
        args += list(before[i])
    scratch = [
        pltpu.VMEM((2, 2, 128 * count, TILE), f32),
        pltpu.SemaphoreType.DMA((2, 2 * count * TILE // 128)),
    ]
    if last:
        in_specs += [whole(*m.shape) for m in mats] + [whole(512, 512), pl.BlockSpec(memory_space=pltpu.SMEM)]
        args = in_hbm(*args, *mats, et) + [core]
        out_shape = [jax.ShapeDtypeStruct((64 * 40, 128), f32)] * 2
        out_specs = [whole(64 * 40, 128)] * 2
        scratch = [pltpu.VMEM(mat_shape, f32)] + scratch
    else:
        out_shape = [jax.ShapeDtypeStruct((128 * count, 2048), bf16)] * 2 + [jax.ShapeDtypeStruct(mat_shape, f32)]
        out_specs = [cols(128 * count)] * 2 + [whole(*mat_shape)]
    return pl.pallas_call(
        functools.partial(overlap_kernel, k),
        grid=(2048 // TILE,),
        out_shape=out_shape,
        in_specs=in_specs,
        out_specs=out_specs,
        scratch_shapes=scratch,
        compiler_params=pltpu.CompilerParams(vmem_limit_bytes=(30 if last else 60) << 20),
        cost_estimate=pl.CostEstimate(flops=8 << 30, bytes_accessed=8 << 20, transcendentals=0),
        name="overlap",
    )(*args)


def rotate_kernel(*refs):
    n = len(CHUNKS)
    e_ref, rot_ref, rota_ref, e3, xbuf, sems = refs[n:]

    @pl.when(pl.program_id(0) == 0)
    def _():
        hi, lo = halves(e_ref[...])
        e3[:, :512] = hi
        e3[:, 512:1024] = hi
        e3[:, 1024:] = lo

    (fh, fl), (ah, al) = load_tile(refs[:n], CHUNKS, xbuf, sems)
    rot_ref[...] = nn(e3[...], jnp.concatenate([fh, fl, fh], 0))
    rota_ref[...] = nn(e3[...], jnp.concatenate([ah, al, ah], 0))


def run_rotate(got, et):
    f32 = jnp.float32
    return pl.pallas_call(
        rotate_kernel,
        grid=(2048 // TILE,),
        out_shape=[jax.ShapeDtypeStruct((512, 2048), f32)] * 2,
        in_specs=[pl.BlockSpec(memory_space=pl.ANY)] * len(got) + [whole(512, 512)],
        out_specs=[cols(512)] * 2,
        scratch_shapes=[
            pltpu.VMEM((512, 1536), jnp.bfloat16),
            pltpu.VMEM((2, 2, 512, TILE), f32),
            pltpu.SemaphoreType.DMA((2, 8 * TILE // 128)),
        ],
        compiler_params=pltpu.CompilerParams(vmem_limit_bytes=60 << 20),
        cost_estimate=pl.CostEstimate(flops=16 << 30, bytes_accessed=16 << 20, transcendentals=0),
        name="rotate",
    )(*got, et)


def finish_kernel(pay_ref, rot_ref, rota_ref, gram_ref, ham_ref, ritz_ref, res_ref, tot, scale):
    @pl.when(pl.program_id(0) == 0)
    def _():
        tot[...] = jnp.sum(pay_ref[...], axis=0)
        ritz = tot[32:36, :] / (tot[36:40, :] + quot_eps)
        ritz_ref[...] = ritz
        turned = jnp.concatenate([ritz, ritz], 0).T
        for q in range(4):
            scale[128 * q : 128 * q + 128, :] = jnp.broadcast_to(turned[:, q : q + 1], (128, 128))

    ritz = scale[pl.ds(pl.multiple_of(pl.program_id(0) * FINISH, FINISH), FINISH), :]
    for c in range(2048 // 128):
        at = slice(128 * c, 128 * c + 128)
        res_ref[:, at] = rota_ref[:, at] - ritz * rot_ref[:, at]

    @pl.when(pl.program_id(0) == pl.num_programs(0) - 1)
    def _():
        row = lax.broadcasted_iota(jnp.int32, (512, 512), 0)
        col = lax.broadcasted_iota(jnp.int32, (512, 512), 1)
        perm = jnp.where(4 * (row & 127) + (row >> 7) == col, 1.0, 0.0).astype(jnp.bfloat16)
        parts = split3(jnp.concatenate([tot[pl.ds(q, 8, stride=4), :] for q in range(4)], 1))
        mats = (nn(parts[:, :512], perm) + nn(parts[:, 512:1024], perm)) + nn(parts[:, 1024:], perm)
        gram_ref[...] = mats[:4]
        ham_ref[...] = mats[4:]


def run_finish(pay, rot, rota):
    f32 = jnp.float32
    block = pl.BlockSpec((FINISH, 2048), lambda t: (t, 0))
    return pl.pallas_call(
        finish_kernel,
        grid=(512 // FINISH,),
        out_shape=(
            jax.ShapeDtypeStruct((4, 512), f32),
            jax.ShapeDtypeStruct((4, 512), f32),
            jax.ShapeDtypeStruct((4, 128), f32),
            jax.ShapeDtypeStruct((512, 2048), f32),
        ),
        in_specs=[whole(64, 40, 128), block, block],
        out_specs=(whole(4, 512), whole(4, 512), whole(4, 128), block),
        scratch_shapes=[pltpu.VMEM((40, 128), f32), pltpu.VMEM((512, 128), f32)],
        compiler_params=pltpu.CompilerParams(vmem_limit_bytes=24 << 20),
        cost_estimate=pl.CostEstimate(flops=8 << 20, bytes_accessed=16 << 20, transcendentals=0),
        name="finish",
    )(pay, *in_hbm(rot, rota))


def on_device(orbitals, potential, cutoff, eigvec):
    orb = orbitals.reshape(4, 2048, 128).transpose(1, 0, 2).reshape(8, 8, 32, 4, 128)
    pot = potential.reshape(8, 8, 32, 128)
    et = eigvec.reshape(128, 4, 512).transpose(2, 1, 0).reshape(512, 512)
    core = lax.axis_index("core").astype(jnp.int32).reshape(1)
    gots, before, mats = [], [], []
    for k, count in enumerate(CHUNKS):
        sent = run_filter(orb, pot, cutoff, sum(CHUNKS[:k]), count).reshape(128, 32 * count, 128)
        gots.append(lax.all_to_all(sent, AXES, split_axis=0, concat_axis=0, tiled=True))
        out = run_overlap(k, gots[k], before, mats, et, core)
        if k < len(CHUNKS) - 1:
            before.append(out[:2])
            mats.append(out[2])
    keep, send = out
    pay = (keep + lax.ppermute(send, "core", [(0, 1), (1, 0)])).reshape(64, 40, 128)
    pay, gots[-1] = lax.optimization_barrier((pay, gots[-1]))
    pay = lax.all_to_all(pay, ("oh", "pt"), split_axis=0, concat_axis=0, tiled=True)
    rotated, rot_applied = run_rotate(gots, et)
    gram, hamil_sub, ritz, residual = run_finish(pay, rotated, rot_applied)
    return (gram, hamil_sub, rotated, residual, ritz.reshape(512))


def solution(mesh):
    fine = jax.sharding.Mesh(np.asarray(mesh.devices).reshape(8, 2, 8), AXES)
    return jax.shard_map(
        on_device,
        mesh=fine,
        in_specs=(P(AXES, None), P(), P(), P()),
        out_specs=(P(AXES, None), P(AXES, None), P(None, AXES), P(None, AXES), P()),
        check_vma=False,
    )
```
